32 devices in a mesh: ctx: 16 (over z, y, x), srv: 2 (over core).
Axes of the slice: x: 2, y: 2, z: 4, core: 2. Of those that a mesh axis runs over, the one named last changes fastest.
Arguments:
- tokens: bfloat16 [4096, 2048], P('ctx'), may hold values from -6 to 6
- norm_gain: float32 [2048], replicated, may hold values from 0.5 to 2
- q_gain: float32 [128], replicated, may hold values from 0.7 to 16
- k_gain: float32 [128], replicated, may hold values from 0.7 to 16
- w_query: bfloat16 [2048, 2048], P(None, 'srv'), may hold values from -0.125 to 0.125
- w_key: bfloat16 [2048, 256], replicated, may hold values from -0.125 to 0.125
- w_value: bfloat16 [2048, 256], replicated, may hold values from -0.125 to 0.125
- w_out: bfloat16 [2048, 2048], P('srv'), may hold values from -0.125 to 0.125
- doc_lengths: int32 [4], replicated, may hold values from 1 to 2560, 4096 in all
- stretch_offsets: int32 [16], P('ctx'), may hold values from 0 to 5880, as said below
Outputs:
- attn_out: bfloat16 [4096, 2048], P(('ctx', 'srv'))
The draws below stay inside these ranges and needn't reach their ends.
Inputs may be any that keep to these rules, and one draw needn't show every extreme that they name: `doc_lengths`: the lengths sum to 4096; the longest is exactly 2560. `stretch_offsets`: offsets rise from block to block by 256 to 511; the first is below 256; the last is exactly (15) * 256 + 8 * 255.
All inputs are finite; a program needn't handle non-finite values.
Results may differ from the reference program's by a relative error of at most 0.013.
The reference program's roundings to bfloat16 on the way count: a program that leaves them out, or rounds other values in their place, can miss the bound.
Values may be sent and summed in bfloat16 or wider, within the bound.
No kernel may reach another device: no remote copies, remote signals or barrier semaphores. Data moves between devices by JAX's collectives and lax.ppermute only.
A program may use at most 128 MiB of HBM per device.

```python
import math
import jax
import jax.numpy as jnp
import numpy as np
from jax import lax

D = 2048
HEAD_DIM = 128
QH = 16
KVH = 2
TOK_CTX = 256
DOCS = 4
TOKENS = 4096
MOST_LEN = 2560
N_CTX = 16


def gain_values(key, lowest, highest):
    uniform_draw = jax.random.uniform(key, (HEAD_DIM,), jnp.float32)
    return jnp.exp(jnp.log(lowest) + uniform_draw * (jnp.log(highest) - jnp.log(lowest)))


def draw_q_gain(key, part):
    folded = jax.random.fold_in(key, 17)
    return gain_values(folded, 0.7, 2.5)


def draw_k_gain(key, part):
    folded = jax.random.fold_in(key, 29)
    return gain_values(folded, 0.7, 2.5)


def draw_stretch_offsets(key, part):
    folded = jax.random.fold_in(key, 41)
    first_gaps = jax.random.randint(folded, (N_CTX // 2,), 0, TOK_CTX, dtype=jnp.int32)
    second_gaps = TOK_CTX - 1 - first_gaps
    gap_sizes = jnp.stack([first_gaps, second_gaps], axis=1).reshape(N_CTX)
    return (jnp.cumsum(gap_sizes).astype(jnp.int32) + jnp.arange(N_CTX, dtype=jnp.int32) * TOK_CTX).astype(jnp.int32)


def levels(stream_key, shape, split, least, largest):
    def one(dim, shards_of):
        heights = jax.random.uniform(jax.random.fold_in(jax.random.fold_in(stream_key, 6), dim), (shards_of,), jnp.float32, least / len(split), largest / len(split))
        return jnp.repeat(jnp.exp(heights), shape[dim] // shards_of).reshape((-1,) + (1,) * (len(shape) - dim - 1))

    factor_of = one(*split[0])
    for cut in split[1:]:
        factor_of = factor_of * one(*cut)
    return factor_of


def split_up(count, total, most, slope):
    portions = [(1 << 20) // math.isqrt(rank ** slope) + 1 for rank in range(2, count + 1)]
    spare, given = total - most - (count - 1), [1] * (count - 1)
    while spare > 0:
        candidates = [i for i in range(count - 1) if given[i] < most]
        mass, budget = sum([portions[i] for i in candidates]), spare
        for i in candidates:
            extra = min(most - given[i], max(1, budget * portions[i] // mass), spare)
            given[i] = given[i] + extra
            spare = spare - extra
    return np.array([most] + given)


def uneven(own_key, amount, total, most, slope):
    if amount == 2:
        one = jax.random.randint(own_key, (), max(1, total - most), min(most, total - 1) + 1)
        return jnp.stack([one, total - one])
    lengths = jnp.asarray(split_up(amount, total, most, slope), jnp.int32)
    twos = (amount - 1) // 2
    source_of, taker = lengths[1:1 + 2 * twos:2], lengths[2:2 + 2 * twos:2]
    room = jnp.minimum(source_of - 1, most - taker)
    shifted = jax.random.randint(jax.random.fold_in(own_key, 1), (twos,), 0, 1 << 20) % (room + 1)
    lengths = lengths.at[1:1 + 2 * twos:2].set(source_of - shifted).at[2:2 + 2 * twos:2].set(taker + shifted)
    return lengths[jax.random.permutation(jax.random.fold_in(own_key, 2), amount)]


def gaussian(rng, shape, deviation, limit, split=(), kind=jnp.bfloat16):
    drawn = jax.random.normal(rng, shape, jnp.float32) * deviation
    if len(split) > 0:
        drawn = levels(rng, shape, split, -0.22, 0.18) * drawn
    return jnp.clip(drawn, min=-limit, max=limit).astype(kind)


def setup_inputs(seed: int = 0) -> dict:
    keys = jax.random.split(jax.random.key(seed), 11)
    tokens = gaussian(keys[0], (TOKENS, D), 1.0, 6.0, ((0, 16),))
    norm_gain = jnp.clip(jnp.exp(jax.random.uniform(keys[1], (D,), jnp.float32, math.log(0.5), math.log(2.0))), 0.5, 2.0)
    q_gain = draw_q_gain(jax.random.fold_in(keys[10], 71), 0)
    k_gain = draw_k_gain(jax.random.fold_in(keys[10], 71), 0)
    w_query = gaussian(keys[4], (D, QH * HEAD_DIM), D ** -0.5, 0.125, ((1, 2),))
    w_key = gaussian(keys[5], (D, KVH * HEAD_DIM), D ** -0.5, 0.125)
    w_value = gaussian(keys[6], (D, KVH * HEAD_DIM), D ** -0.5, 0.125)
    w_out = gaussian(keys[7], (QH * HEAD_DIM, D), (QH * HEAD_DIM) ** -0.5, 0.125, ((0, 2),))
    doc_lengths = uneven(keys[8], DOCS, TOKENS, MOST_LEN, 2).astype(jnp.int32)
    stretch_offsets = draw_stretch_offsets(jax.random.fold_in(keys[10], 71), 0)
    return {"tokens": tokens, "norm_gain": norm_gain, "q_gain": q_gain, "k_gain": k_gain, "w_query": w_query, "w_key": w_key, "w_value": w_value, "w_out": w_out, "doc_lengths": doc_lengths, "stretch_offsets": stretch_offsets}


rope_base = 1000000.0
norm_eps = 1e-06
masked_score = -1e+30

def rms_scale(values, weights):
    mean_square = lax.optimization_barrier(jnp.mean(values * values, axis=-1, keepdims=True))
    return values * lax.rsqrt(mean_square + norm_eps) * weights

def rotate(values, positions):
    half_dim = values.shape[-1] // 2
    frequency = rope_base ** (-2.0 * jnp.arange(half_dim, dtype=jnp.float32) / values.shape[-1])
    angles = positions.astype(jnp.float32)[:, None] * frequency[None, :]
    cosine = jnp.cos(angles)[:, None, :]
    sine_part = jnp.sin(angles)[:, None, :]
    first_half = values[..., :half_dim]
    second_half = values[..., half_dim:]
    return jnp.concatenate([first_half * cosine - second_half * sine_part, second_half * cosine + first_half * sine_part], axis=-1)

def segment_of(indices, doc_ends):
    return lax.optimization_barrier(jnp.sum((indices[None, :] >= doc_ends[:, None]).astype(jnp.int32), axis=0))

def reference(tokens, norm_gain, q_gain, k_gain, w_query, w_key, w_value, w_out, doc_lengths, stretch_offsets):
    total_rows = tokens.shape[0]
    group_size = QH // KVH
    score_scale = HEAD_DIM ** (-0.5)
    normed = rms_scale(tokens.astype(jnp.float32), norm_gain).astype(jnp.bfloat16)
    all_index = jnp.arange(total_rows, dtype=jnp.int32)
    positions = (stretch_offsets[all_index // TOK_CTX] + all_index % TOK_CTX).astype(jnp.int32)
    doc_ends = jnp.cumsum(doc_lengths).astype(jnp.int32)
    segments = segment_of(all_index, doc_ends)
    queries = jnp.dot(normed, w_query, preferred_element_type=jnp.float32).reshape(total_rows, QH, HEAD_DIM)
    queries = rotate(rms_scale(queries, q_gain), positions).astype(jnp.bfloat16)
    queries = lax.optimization_barrier(queries).reshape(total_rows, KVH, group_size, HEAD_DIM)
    keys_all = jnp.dot(normed, w_key, preferred_element_type=jnp.float32).reshape(total_rows, KVH, HEAD_DIM)
    keys_all = rotate(rms_scale(keys_all, k_gain), positions).astype(jnp.bfloat16)
    keys_wide = lax.optimization_barrier(keys_all).astype(jnp.float32)
    values_all = jnp.dot(normed, w_value, preferred_element_type=jnp.float32).astype(jnp.bfloat16)
    values_all = lax.optimization_barrier(values_all).astype(jnp.float32).reshape(total_rows, KVH, HEAD_DIM)
    block_rows = math.gcd(total_rows, 512)

    def attend(block_start):
        query_block = lax.dynamic_slice_in_dim(queries, block_start, block_rows, 0).astype(jnp.float32)
        query_index = block_start + jnp.arange(block_rows, dtype=jnp.int32)
        query_segment = lax.dynamic_slice_in_dim(segments, block_start, block_rows, 0)
        allowed = (query_segment[:, None] == segments[None, :]) & (all_index[None, :] <= query_index[:, None])
        scores = jnp.einsum('tkgd,pkd->kgtp', query_block, keys_wide) * score_scale
        scores = jnp.where(allowed[None, None], scores, masked_score)
        top_score = lax.optimization_barrier(jnp.max(scores, axis=-1, keepdims=True))
        exponent = jnp.where(allowed[None, None], jnp.exp(scores - top_score), 0.0)
        denominator = lax.optimization_barrier(jnp.sum(exponent, axis=-1))
        weights = lax.optimization_barrier(exponent.astype(jnp.bfloat16)).astype(jnp.float32)
        mixed_heads = jnp.einsum('kgtp,pkd->kgtd', weights, values_all) / denominator[..., None]
        return jnp.transpose(mixed_heads, (2, 0, 1, 3)).reshape(block_rows, QH * HEAD_DIM)
    starts = jnp.arange(total_rows // block_rows, dtype=jnp.int32) * block_rows
    attended = lax.map(attend, starts).reshape(total_rows, QH * HEAD_DIM).astype(jnp.bfloat16)
    return jnp.dot(attended, w_out, preferred_element_type=jnp.float32).astype(jnp.bfloat16)
```

```python
import functools

import jax
import jax.numpy as jnp
from jax import lax
from jax.experimental import pallas as pl
from jax.experimental.pallas import tpu as pltpu
from jax.sharding import PartitionSpec as P

rope_base = 1000000.0
norm_eps = 1e-06
masked_score = -1e30
log2_e = 1.4426950408889634
PLANE = 4


ANY = pl.BlockSpec(memory_space=pl.ANY)
VMEM = pl.BlockSpec(memory_space=pltpu.VMEM)
SMEM = pl.BlockSpec(memory_space=pltpu.SMEM)


def rope_table(offset, rows, head_dim):
    half_dim = head_dim // 2
    frequency = rope_base ** (-2.0 * jnp.arange(half_dim, dtype=jnp.float32) / head_dim)
    positions = (offset + jnp.arange(rows, dtype=jnp.int32)).astype(jnp.float32)
    angles = positions[:, None] * frequency[None, :]
    cosine, sine = jnp.cos(angles), jnp.sin(angles)
    return jnp.concatenate([cosine, cosine], 1), jnp.concatenate([-sine, sine], 1)


def norm_rotate(x, gain, cosine, sine):
    mean_square = jnp.mean(x * x, axis=-1, keepdims=True)
    x = x * lax.rsqrt(mean_square + norm_eps) * gain
    return x * cosine + pltpu.roll(x, x.shape[-1] // 2, 1) * sine


def kv_kernel(
    head, tokens, norm_gain, w_key, w_value, k_gain, cosine, sine, normed_out, kv_out
):
    rows, head_dim = cosine.shape
    x = tokens[...].astype(jnp.float32)
    mean_square = jnp.mean(x * x, axis=-1, keepdims=True)
    normed = (x * lax.rsqrt(mean_square + norm_eps) * norm_gain[...]).astype(jnp.bfloat16)
    normed_out[...] = normed
    keys = jnp.dot(normed, w_key[...], preferred_element_type=jnp.float32)
    values = jnp.dot(normed, w_value[...], preferred_element_type=jnp.float32)
    kv_out[:rows] = norm_rotate(keys, k_gain[...], cosine[...], sine[...]).astype(
        jnp.bfloat16
    )
    kv_out[rows:] = values.astype(jnp.bfloat16)


def project_kv(head, tokens, norm_gain, w_key, w_value, k_gain, cosine, sine):
    rows, width = tokens.shape
    head_dim = cosine.shape[1]
    whole = lambda a: pl.BlockSpec(a.shape, lambda i, h: (0, 0))
    column = pl.BlockSpec((width, head_dim), lambda i, h: (0, h[0]))
    return pl.pallas_call(
        kv_kernel,
        grid_spec=pltpu.PrefetchScalarGridSpec(
            num_scalar_prefetch=1,
            grid=(1,),
            in_specs=[
                whole(tokens),
                whole(norm_gain),
                column,
                column,
                whole(k_gain),
                whole(cosine),
                whole(sine),
            ],
            out_specs=[
                pl.BlockSpec((rows, width), lambda i, h: (0, 0)),
                pl.BlockSpec((2 * rows, head_dim), lambda i, h: (0, 0)),
            ],
        ),
        out_shape=[
            jax.ShapeDtypeStruct((rows, width), jnp.bfloat16),
            jax.ShapeDtypeStruct((2 * rows, head_dim), jnp.bfloat16),
        ],
        name="project_kv",
    )(head, tokens, norm_gain, w_key, w_value, k_gain, cosine, sine)


def q_kernel(normed, w_query, q_gain, cosine, sine, q_out):
    head_dim = cosine.shape[1]
    queries = jnp.dot(normed[...], w_query[...], preferred_element_type=jnp.float32)
    for h in range(q_out.shape[0]):
        x = queries[:, h * head_dim : (h + 1) * head_dim]
        q_out[h] = norm_rotate(x, q_gain[...], cosine[...], sine[...]).astype(jnp.bfloat16)


def project_q(normed, w_query, q_gain, cosine, sine, per_step=2):
    rows, width = normed.shape
    head_dim = cosine.shape[1]
    heads = w_query.shape[1] // head_dim
    whole = lambda a: pl.BlockSpec(a.shape, lambda i: (0, 0))
    return pl.pallas_call(
        q_kernel,
        grid=(heads // per_step,),
        in_specs=[
            whole(normed),
            pl.BlockSpec((width, per_step * head_dim), lambda i: (0, i)),
            whole(q_gain),
            whole(cosine),
            whole(sine),
        ],
        out_specs=pl.BlockSpec((per_step, rows, head_dim), lambda i: (i, 0, 0)),
        out_shape=jax.ShapeDtypeStruct((heads, rows, head_dim), jnp.bfloat16),
        cost_estimate=pl.CostEstimate(
            flops=2 * rows * width * heads * head_dim,
            bytes_accessed=2 * width * heads * head_dim,
            transcendentals=0,
        ),
        name="project_q",
    )(normed, w_query, q_gain, cosine, sine)


def attend_kernel(distances, near, scale, info, q, *refs):
    pieces = refs[: len(distances)]
    out, keys, values, top, total, mixed, sems = refs[len(distances) :]
    heads, rows, head_dim = q.shape
    docs = info.shape[0] - 2
    index, far = info[docs], info[docs + 1]
    planes = 1 + max(s for group, _ in distances for s in group)
    last = planes - 1
    lane = lax.rem(index, PLANE)
    own_slot = PLANE * last + lane
    base_block = index - own_slot

    def copies(is_far):
        for n, (group, mate) in enumerate(distances):
            for place, s in enumerate(group):
                if (s > near) != is_far:
                    continue
                slot = PLANE * (last - s) + lax.bitwise_xor(lane, jnp.int32(mate))
                at = pl.ds(pl.multiple_of(slot * rows, rows), rows)
                for part, buffer in enumerate((keys, values)):
                    from_row = (2 * place + part) * rows
                    yield pltpu.make_async_copy(
                        pieces[n].at[pl.ds(from_row, rows)],
                        buffer.at[at],
                        sems.at[n, 2 * place + part],
                    )

    far_copies = list(copies(True))
    near_copies = list(copies(False))
    for c in near_copies:
        c.start()

    first_token = index * rows
    first_start = jnp.int32(0)
    final_start = jnp.int32(0)
    token = first_token + lax.broadcasted_iota(jnp.int32, (rows, head_dim), 0)
    start = jnp.zeros((rows, head_dim), jnp.int32)
    end = jnp.int32(0)
    for d in range(docs):
        end = end + info[d]
        first_start = jnp.where(end <= first_token, end, first_start)
        final_start = jnp.where(end <= first_token + rows - 1, end, final_start)
        start = jnp.where(end <= token, end, start)

    if far_copies:

        @pl.when(far > 0)
        def _():
            for c in far_copies:
                c.start()
            for c in far_copies:
                c.wait()

    for c in near_copies:
        c.wait()

    span = 2 * rows
    tiles = span // head_dim
    wide = lambda a: jnp.concatenate([a] * tiles, axis=1)

    def chunk(c, masked, first):
        at = pl.ds(pl.multiple_of(c * span, span), span)
        key, value = keys[at], values[at]
        if masked:
            u = (base_block * rows + c * span) + lax.broadcasted_iota(
                jnp.int32, (rows, span), 1
            )
            allowed = (u >= wide(start)) & (u <= wide(token))
        for h in range(heads):
            score = lax.dot_general(
                q[h], key, (((1,), (1,)), ((), ())), preferred_element_type=jnp.float32
            )
            if masked:
                score = jnp.where(allowed, score, masked_score)
            high = jnp.max(score, axis=1, keepdims=True) * scale
            high = jnp.broadcast_to(high, (rows, head_dim))
            if not first:
                old = top[h]
                high = jnp.maximum(high, old)
                factor = jnp.exp2(old - high)
            weight = jnp.exp2(score * scale - wide(high))
            part = weight[:, :head_dim]
            for n in range(1, tiles):
                part = part + weight[:, n * head_dim : (n + 1) * head_dim]
            product = jnp.dot(
                weight.astype(jnp.bfloat16), value, preferred_element_type=jnp.float32
            )
            top[h] = high
            if first:
                total[h] = part
                mixed[h] = product
            else:
                total[h] = total[h] * factor + part
                mixed[h] = mixed[h] * factor + product

    last_chunk = own_slot // 2
    first_chunk = (lax.div(first_start, rows) - base_block) // 2
    chunk(last_chunk, True, True)

    def step(n, _):
        c = last_chunk - 1 - n
        needs_mask = (base_block * rows + c * span) < final_start

        @pl.when(needs_mask)
        def _():
            chunk(c, True, False)

        @pl.when(jnp.logical_not(needs_mask))
        def _():
            chunk(c, False, False)

        return 0

    lax.fori_loop(0, last_chunk - first_chunk, step, 0)
    for h in range(heads):
        denominator = jnp.sum(total[h], axis=1, keepdims=True)
        out[:, h * head_dim : (h + 1) * head_dim] = (mixed[h] / denominator).astype(
            jnp.bfloat16
        )


def attend(info, q, pieces, distances, near):
    heads, rows, head_dim = q.shape
    planes = 1 + max(s for group, _ in distances for s in group)
    depth = max(len(group) for group, _ in distances)
    return pl.pallas_call(
        functools.partial(attend_kernel, distances, near, head_dim**-0.5 * log2_e),
        in_specs=[SMEM, VMEM] + [ANY] * len(pieces),
        out_specs=VMEM,
        out_shape=jax.ShapeDtypeStruct((rows, heads * head_dim), jnp.bfloat16),
        scratch_shapes=[
            pltpu.VMEM((planes * PLANE * rows, head_dim), jnp.bfloat16),
            pltpu.VMEM((planes * PLANE * rows, head_dim), jnp.bfloat16),
            pltpu.VMEM((heads, rows, head_dim), jnp.float32),
            pltpu.VMEM((heads, rows, head_dim), jnp.float32),
            pltpu.VMEM((heads, rows, head_dim), jnp.float32),
            pltpu.SemaphoreType.DMA((len(pieces), 2 * depth)),
        ],
        name="attend",
    )(info, q, *pieces)


def local(
    tokens, norm_gain, q_gain, k_gain, w_query, w_key, w_value, w_out, doc_lengths, stretch_offsets
):
    rows = tokens.shape[0]
    head_dim = q_gain.shape[0]
    server = lax.axis_index("srv")
    index = lax.axis_index("ctx")
    servers = lax.axis_size("srv")
    count = lax.axis_size("ctx")
    cosine, sine = rope_table(stretch_offsets[0], rows, head_dim)
    normed, own = project_kv(
        server.reshape(1).astype(jnp.int32),
        tokens,
        norm_gain[None],
        w_key,
        w_value,
        k_gain[None],
        cosine,
        sine,
    )
    queries = project_q(normed, w_query, q_gain[None], cosine, sine)

    def mate(block, m):
        return lax.ppermute(block, "ctx", [(i, i ^ m) for i in range(count)])

    def onward(block):
        return lax.ppermute(block, "ctx", [(i, (i + PLANE) % count) for i in range(count)])

    total_tokens = rows * count
    longest = total_tokens // 2 + total_tokens // 8
    reach = (longest + rows - 2) // rows
    near = min(reach // PLANE, count // PLANE - 1)
    most = min((reach + PLANE - 1) // PLANE, count // PLANE - 1)
    pieces, distances = [], []
    behind = own
    passed = []
    for s in range(near):
        behind = onward(behind)
        passed.append(behind)
    for m in range(PLANE):
        pieces.append(mate(own, m) if m else own)
        distances.append(((0,), m))
    passed = jnp.concatenate(passed, 0)
    for m in range(PLANE):
        pieces.append(mate(passed, m) if m else passed)
        distances.append((tuple(range(1, near + 1)), m))
    far = jnp.int32(0)
    if most > near:
        ends = jnp.cumsum(doc_lengths)
        begins = ends - doc_lengths
        spread = (ends - 1) // (rows * PLANE) - begins // (rows * PLANE)
        far = jnp.max(spread) > near

        def fetch(block):
            block = onward(block)
            return tuple(mate(block, m) if m else block for m in range(PLANE))

        got = lax.cond(far, fetch, lambda block: (block,) * PLANE, behind)
        for m in range(PLANE):
            pieces.append(got[m])
            distances.append(((near + 1,), m))
        far = far.astype(jnp.int32)
    info = jnp.concatenate(
        [doc_lengths, index.reshape(1).astype(jnp.int32), far.reshape(1)]
    )
    attended = attend(info, queries, pieces, distances, near)
    share = rows // servers
    other = lax.dynamic_slice_in_dim(attended, (1 - server) * share, share, 0)
    mine = lax.dynamic_slice_in_dim(attended, server * share, share, 0)
    sent = jnp.dot(other, w_out, preferred_element_type=jnp.float32).astype(jnp.bfloat16)
    received = lax.ppermute(sent, "srv", [(0, 1), (1, 0)])
    kept = jnp.dot(mine, w_out, preferred_element_type=jnp.float32)
    return (kept + received.astype(jnp.float32)).astype(jnp.bfloat16)


def solution(mesh):
    return jax.shard_map(
        local,
        mesh=mesh,
        in_specs=(
            P("ctx", None),
            P(),
            P(),
            P(),
            P(None, "srv"),
            P(),
            P(),
            P("srv", None),
            P(),
            P("ctx"),
        ),
        out_specs=P(("ctx", "srv"), None),
        check_vma=False,
    )
```
